256 devices in a mesh: grp: 4 (over z_hi), seq: 16 (over z_lo, y, core), dp: 4 (over x).
Axes of the slice: x: 4, y: 4, z: 8 (z_hi: 4, z_lo: 2; z = z_hi * 2 + z_lo), core: 2. Of those that a mesh axis runs over, the one named last changes fastest.
Arguments:
- text_hidden: bfloat16 [16, 256, 4096], P(('grp', 'dp'), 'seq'), may hold values from -6 to 6
- text_lengths: int32 [16], P(('grp', 'dp')), may hold values from 32 to 256, as said below
- norm_gain: bfloat16 [4096], replicated, may hold values from 0.5 to 1.5
- t5_gate: bfloat16 [4096, 10240], P('grp', 'seq'), may hold values from -0.09375 to 0.09375
- t5_up: bfloat16 [4096, 10240], P('grp', 'seq'), may hold values from -0.09375 to 0.09375
- t5_down: bfloat16 [10240, 4096], P('seq', 'grp'), may hold values from -0.0625 to 0.0625
- final_gain: bfloat16 [4096], replicated, may hold values from 0.5 to 1.5
- text_proj: bfloat16 [4096, 16, 384], P(None, 'seq'), may hold values from -0.09375 to 0.09375
- image_qkv: bfloat16 [16, 2048, 3, 2048], P(('grp', 'dp'), 'seq'), may hold values from -6 to 6
- grad_image: bfloat16 [16, 2048, 2048], P(('grp', 'dp'), 'seq'), may hold values from -192 to 192
- grad_text: bfloat16 [16, 256, 2048], P(('grp', 'dp'), 'seq'), may hold values from -192 to 192
Outputs:
- image_grad: bfloat16 [16, 2048, 3, 16, 128], P(('grp', 'dp'), None, None, 'seq')
- proj_grad: float32 [4096, 16, 384], P(('grp', 'dp'), 'seq')
The draws below stay inside these ranges and needn't reach their ends.
Inputs may be any that keep to these rules, and one draw needn't show every extreme that they name: text_lengths[b] real prompt tokens in sample b, the rest padding; one sample has 256 and one has 32.
All inputs are finite; a program needn't handle non-finite values.
Results may differ from the reference program's by a relative error of at most 0.024.
Values may be sent and summed in bfloat16 or wider, within the bound.
No kernel may reach another device: no remote copies, remote signals or barrier semaphores. Data moves between devices by JAX's collectives and lax.ppermute only.
A program may use at most 128 MiB of HBM per device.

```python
from functools import partial
import jax
import jax.numpy as jnp
from jax import lax

HEADS = 16
HD = 128
DT5 = 4096
FFT5 = 10240
IMG = 2048
TXT = 256
SAMPLES = 16


def draw_text_lengths(key, part):
    first_key, second_key, third_key = jax.random.split(key, 3)
    lengths = jax.random.randint(first_key, (SAMPLES,), TXT // 8, TXT + 1)
    longest = jax.random.randint(second_key, (), 0, SAMPLES)
    shortest = (longest + jax.random.randint(third_key, (), 1, SAMPLES)) % SAMPLES
    order = jnp.arange(SAMPLES)
    lengths = jnp.where(order == longest, TXT, lengths)
    lengths = jnp.where(order == shortest, TXT // 8, lengths)
    return lengths.astype(jnp.int32)


def draw_image_qkv(key, part):
    base_key = jax.random.fold_in(key, 0)
    full_shape = (SAMPLES, IMG, 3, HEADS, HD)
    values = jnp.clip(jax.random.normal(base_key, full_shape, jnp.float32), -6.0, 6.0)
    return values.reshape(SAMPLES, IMG, 3, HEADS * HD).astype(jnp.bfloat16)


def steps_of(stream_key, shape, pieces, least, high):
    def one(axis_at, shards_of):
        heights = jax.random.uniform(jax.random.fold_in(jax.random.fold_in(stream_key, 6), axis_at), (shards_of,), jnp.float32, least / len(pieces), high / len(pieces))
        return jnp.repeat(jnp.exp(heights), shape[axis_at] // shards_of).reshape((-1,) + (1,) * (len(shape) - axis_at - 1))

    loudness = one(*pieces[0])
    for cut in pieces[1:]:
        loudness = loudness * one(*cut)
    return loudness


def gaussian(rng, shape, width, bound, pieces=(), kind=jnp.bfloat16):
    result = width * jax.random.normal(rng, shape, jnp.float32)
    if pieces:
        result = result * steps_of(rng, shape, pieces, -0.22, 0.18)
    return jnp.clip(result, -bound, bound).astype(kind)


def setup_inputs(seed: int = 0) -> dict:
    streams_of = jax.random.split(jax.random.key(seed), 12)
    text_hidden = gaussian(streams_of[0], (SAMPLES, TXT, DT5), 1.0, 6.0, ((0, 16), (1, 16)))
    text_lengths = draw_text_lengths(jax.random.fold_in(streams_of[11], 71), 0)
    norm_gain = jnp.clip(1.0 + 0.1 * jax.random.normal(streams_of[2], (DT5,), jnp.float32), 0.5, 1.5).astype(jnp.bfloat16)
    t5_gate = gaussian(streams_of[3], (DT5, FFT5), DT5 ** -0.5, 0.09375, ((0, 4), (1, 16)))
    t5_up = gaussian(streams_of[4], (DT5, FFT5), DT5 ** -0.5, 0.09375, ((0, 4), (1, 16)))
    t5_down = gaussian(streams_of[5], (FFT5, DT5), FFT5 ** -0.5, 0.0625, ((0, 16), (1, 4)))
    final_gain = jnp.clip(1.0 + 0.1 * jax.random.normal(streams_of[6], (DT5,), jnp.float32), 0.5, 1.5).astype(jnp.bfloat16)
    text_proj = gaussian(streams_of[7], (DT5, HEADS, 3 * HD), DT5 ** -0.5, 0.09375, ((1, 16),))
    image_qkv = draw_image_qkv(jax.random.fold_in(streams_of[11], 71), 0)
    grad_image = gaussian(streams_of[9], (SAMPLES, IMG, HEADS * HD), 32.0, 192.0, ((0, 16), (1, 16)))
    grad_text = gaussian(streams_of[10], (SAMPLES, TXT, HEADS * HD), 32.0, 192.0, ((0, 16), (1, 16)))
    return {"text_hidden": text_hidden, "text_lengths": text_lengths, "norm_gain": norm_gain, "t5_gate": t5_gate, "t5_up": t5_up, "t5_down": t5_down, "final_gain": final_gain, "text_proj": text_proj, "image_qkv": image_qkv, "grad_image": grad_image, "grad_text": grad_text}


EPSILON = 1e-06
MASKED = -1e+30

def round_low(values):
    return lax.optimization_barrier(values.astype(jnp.bfloat16))

def rms_scale(values, norm_weight):
    mean_square = lax.optimization_barrier(jnp.mean(values * values, axis=-1, keepdims=True))
    return values * lax.rsqrt(mean_square + EPSILON) * norm_weight

def head_reference(key_valid, head_inputs):
    query_rows, key_rows, value_rows, upstream = head_inputs
    query_wide = query_rows.astype(jnp.float32)
    key_wide = key_rows.astype(jnp.float32)
    value_wide = value_rows.astype(jnp.float32)
    upstream_wide = upstream.astype(jnp.float32)
    score_scale = HD ** (-0.5)
    scores = jnp.einsum('qd,kd->qk', query_wide, key_wide) * score_scale
    scores = jnp.where(key_valid[None, :], scores, MASKED)
    row_top = lax.optimization_barrier(jnp.max(scores, axis=1, keepdims=True))
    weights = jnp.exp(scores - row_top)
    softmax_out = weights / lax.optimization_barrier(jnp.sum(weights, axis=1, keepdims=True))
    softmax_low = round_low(softmax_out).astype(jnp.float32)
    attended = round_low(jnp.einsum('qk,kd->qd', softmax_low, value_wide)).astype(jnp.float32)
    row_delta = lax.optimization_barrier(jnp.sum(upstream_wide * attended, axis=1, keepdims=True))
    grad_probs = jnp.einsum('qd,kd->qk', upstream_wide, value_wide)
    grad_scores = round_low(softmax_out * (grad_probs - row_delta)).astype(jnp.float32)
    query_grad = jnp.einsum('qk,kd->qd', grad_scores, key_wide) * score_scale
    key_grad = jnp.einsum('qk,qd->kd', grad_scores, query_wide) * score_scale
    value_grad = jnp.einsum('qk,qd->kd', softmax_low, upstream_wide)
    return jnp.stack([query_grad, key_grad, value_grad], axis=1)

def reference(text_hidden, text_lengths, norm_gain, t5_gate, t5_up, t5_down, final_gain, text_proj, image_qkv, grad_image, grad_text):
    first_gain = norm_gain.astype(jnp.float32)
    second_gain = final_gain.astype(jnp.float32)
    proj_flat = text_proj.reshape(DT5, HEADS * 3 * HD)

    def one_sample(grad_total, sample_inputs):
        hidden, length, qkv_image, upstream_image, upstream_text = sample_inputs
        hidden_wide = hidden.astype(jnp.float32)
        normed = round_low(rms_scale(hidden_wide, first_gain))
        gate_proj = jnp.dot(normed, t5_gate, preferred_element_type=jnp.float32)
        up_proj = jnp.dot(normed, t5_up, preferred_element_type=jnp.float32)
        inner_act = round_low(jax.nn.gelu(gate_proj, approximate=True) * up_proj)
        encoder_ffn = jnp.dot(inner_act, t5_down, preferred_element_type=jnp.float32)
        encoded = round_low(rms_scale(hidden_wide + encoder_ffn, second_gain))
        text_qkv = round_low(jnp.dot(encoded, proj_flat, preferred_element_type=jnp.float32))
        text_qkv = text_qkv.reshape(TXT, HEADS, 3, HD)
        text_valid = jnp.arange(TXT, dtype=jnp.int32) < length
        key_valid = jnp.concatenate([jnp.ones((IMG,), jnp.bool_), text_valid])
        image_heads = qkv_image.reshape(IMG, 3, HEADS, HD)
        upstream_img = upstream_image.reshape(IMG, HEADS, HD)
        upstream_txt = jnp.where(text_valid[:, None, None], upstream_text.reshape(TXT, HEADS, HD), jnp.zeros((), upstream_text.dtype))
        query_all = jnp.concatenate([image_heads[:, 0], text_qkv[:, :, 0]], axis=0)
        key_all = jnp.concatenate([image_heads[:, 1], text_qkv[:, :, 1]], axis=0)
        value_all = jnp.concatenate([image_heads[:, 2], text_qkv[:, :, 2]], axis=0)
        upstream_all = jnp.concatenate([upstream_img, upstream_txt], axis=0)
        per_head = lax.map(partial(head_reference, key_valid), (jnp.moveaxis(query_all, 1, 0), jnp.moveaxis(key_all, 1, 0), jnp.moveaxis(value_all, 1, 0), jnp.moveaxis(upstream_all, 1, 0)))
        all_grads = round_low(per_head)
        image_part = jnp.moveaxis(all_grads[:, :IMG], 0, 2)
        text_part = jnp.moveaxis(all_grads[:, IMG:], 0, 1).reshape(TXT, HEADS * 3 * HD)
        sample_term = lax.dot_general(encoded, text_part, (((0,), (0,)), ((), ())), preferred_element_type=jnp.float32)
        return (grad_total + sample_term, image_part)
    start_total = jnp.zeros((DT5, HEADS * 3 * HD), jnp.float32)
    grad_total, image_grad = lax.scan(one_sample, start_total, (text_hidden, text_lengths, image_qkv, grad_image, grad_text))
    proj_grad = (grad_total / SAMPLES).reshape(DT5, HEADS, 3 * HD)
    return (image_grad, proj_grad)
```

```python
from functools import partial

import jax
import jax.numpy as jnp
from jax import lax
from jax.sharding import PartitionSpec as P

EPSILON = 1e-06
MASKED = -1e30


def rms_scale(values, norm_weight):
    mean_square = jnp.mean(values * values, axis=-1, keepdims=True)
    return values * lax.rsqrt(mean_square + EPSILON) * norm_weight


def shift(x, axis, k):
    n = lax.axis_size(axis)
    return lax.ppermute(x, axis, [(i, (i + k) % n) for i in range(n)])


def shift_y(x, k):
    return lax.ppermute(
        x, "seq", [(i, (i // 8) * 8 + (i % 8 + 2 * k) % 8) for i in range(16)]
    )


def swap_seq(x, bit):
    return lax.ppermute(x, "seq", [(i, i ^ bit) for i in range(16)])


def ring_gather(x, axis):
    half = x.shape[0] // 2
    up = shift(x, axis, 1)
    down = shift(x, axis, -1)
    far_up = shift(up[:half], axis, 1)
    far_down = shift(down[half:], axis, -1)
    return x, up, down, jnp.concatenate([far_up, far_down], axis=0)


def ring_reduce(axis, up_term, down_term):
    up = up_term(1).astype(jnp.bfloat16)
    down = down_term(3).astype(jnp.bfloat16)
    for step in (2, 3):
        up = (shift(up, axis, 1).astype(jnp.float32) + up_term(step)).astype(jnp.bfloat16)
        down = (shift(down, axis, -1).astype(jnp.float32) + down_term(4 - step)).astype(
            jnp.bfloat16
        )
    up = shift(up, axis, 1).astype(jnp.float32) + up_term(0)
    down = shift(down, axis, -1).astype(jnp.float32) + down_term(0)
    return up, down


def gather_seq(x):
    s = lax.axis_index("seq")
    z_lo, y, core = s // 8, (s // 2) % 4, s % 2
    k, r, c = x.shape
    other = swap_seq(x, 8)
    first = jnp.where(z_lo == 0, x, other)
    second = jnp.where(z_lo == 0, other, x)
    pair = jnp.stack([first, second], axis=1)
    up = shift_y(pair, 1)
    down = shift_y(pair, -1)
    far = jnp.stack([shift_y(up[:, 0], 1), shift_y(down[:, 1], -1)], axis=1)
    column = jnp.zeros((k, 2, 4, r, c), x.dtype)
    for block, at in ((pair, y), (up, (y + 3) % 4), (down, (y + 1) % 4), (far, (y + 2) % 4)):
        column = lax.dynamic_update_slice(column, block[:, :, None], (0, 0, at, 0, 0))
    partner = swap_seq(column, 1)
    first = jnp.where(core == 0, column, partner)
    second = jnp.where(core == 0, partner, column)
    return jnp.stack([first, second], axis=3).reshape(k, 16 * r, c)


def head_grads(text_valid, pieces):
    query_img, key_img, value_img, upstream_img, query_txt, key_txt, value_txt, upstream_txt = (
        pieces
    )
    keys_all = jnp.concatenate([key_img, key_txt], axis=0)
    values_all = jnp.concatenate([value_img, value_txt], axis=0)
    key_valid = jnp.concatenate([jnp.ones((key_img.shape[0],), jnp.bool_), text_valid])
    head_dim = query_img.shape[-1]
    score_scale = head_dim ** (-0.5)
    image_rows = query_img.shape[0]
    block_rows = min(image_rows, 512)

    def visit(running, block_pair):
        key_grad, value_grad = running
        query_block, upstream_block = block_pair
        scores = (
            jnp.einsum("qd,kd->qk", query_block, keys_all, preferred_element_type=jnp.float32)
            * score_scale
        )
        scores = jnp.where(key_valid[None, :], scores, MASKED)
        row_top = jnp.max(scores, axis=1, keepdims=True)
        weights = jnp.exp(scores - row_top)
        softmax_out = weights / jnp.sum(weights, axis=1, keepdims=True)
        softmax_low = softmax_out.astype(jnp.bfloat16)
        attended = jnp.dot(softmax_low, values_all, preferred_element_type=jnp.float32).astype(
            jnp.bfloat16
        )
        row_delta = jnp.sum(
            upstream_block.astype(jnp.float32) * attended.astype(jnp.float32), axis=1, keepdims=True
        )
        grad_probs = jnp.einsum(
            "qd,kd->qk", upstream_block, values_all, preferred_element_type=jnp.float32
        )
        grad_scores = (softmax_out * (grad_probs - row_delta)).astype(jnp.bfloat16)
        query_grad = (
            jnp.dot(grad_scores, keys_all, preferred_element_type=jnp.float32) * score_scale
        )
        key_grad = (
            key_grad
            + jnp.einsum("qk,qd->kd", grad_scores, query_block, preferred_element_type=jnp.float32)
            * score_scale
        )
        value_grad = value_grad + jnp.einsum(
            "qk,qd->kd", softmax_low, upstream_block, preferred_element_type=jnp.float32
        )
        return ((key_grad, value_grad), query_grad)

    zero_grads = jnp.zeros(keys_all.shape, jnp.float32)
    image_blocks = (
        query_img.reshape(-1, block_rows, head_dim),
        upstream_img.reshape(-1, block_rows, head_dim),
    )
    running, query_blocks = lax.scan(visit, (zero_grads, zero_grads), image_blocks)
    running, query_txt_grad = visit(running, (query_txt, upstream_txt))
    key_grad, value_grad = running
    query_img_grad = query_blocks.reshape(image_rows, head_dim)
    image_part = jnp.stack(
        [query_img_grad, key_grad[:image_rows], value_grad[:image_rows]], axis=0
    ).astype(jnp.bfloat16)
    text_part = jnp.concatenate(
        [query_txt_grad, key_grad[image_rows:], value_grad[image_rows:]], axis=1
    ).astype(jnp.bfloat16)
    return (image_part, text_part)


def shards(
    text_hidden,
    text_lengths,
    norm_gain,
    t5_gate,
    t5_up,
    t5_down,
    final_gain,
    text_proj,
    image_qkv,
    grad_image,
    grad_text,
):
    g = lax.axis_index("grp")
    d = lax.axis_index("dp")
    first_gain = norm_gain.astype(jnp.float32)
    second_gain = final_gain.astype(jnp.float32)
    local_text = text_hidden[0].astype(jnp.float32)
    rows, width = local_text.shape
    units, chunk = t5_down.shape

    normed = rms_scale(local_text, first_gain).astype(jnp.bfloat16)
    parts = []
    for k in range(4):
        part = lax.dynamic_slice(normed, (0, ((g + k) % 4) * chunk), (rows, chunk))
        parts.append(shift(part, "grp", k) if k else part)
    tokens = gather_seq(jnp.stack(parts, axis=0))
    text_total = tokens.shape[1]

    quarter = units // 4
    mine = lax.dynamic_slice(t5_down, (d * quarter, 0), (quarter, chunk))
    wide = jnp.zeros((quarter, width), jnp.bfloat16)
    for block, off in zip(ring_gather(mine, "grp"), (0, 3, 1, 2)):
        wide = lax.dynamic_update_slice(wide, block, (0, ((g + off) % 4) * chunk))
    down_full = jnp.zeros((units, width), jnp.bfloat16)
    for block, off in zip(ring_gather(wide, "dp"), (0, 3, 1, 2)):
        down_full = lax.dynamic_update_slice(down_full, block, (((d + off) % 4) * quarter, 0))

    def term(weight):
        return lambda k: jnp.dot(tokens[k], weight, preferred_element_type=jnp.float32)

    gate_proj, up_proj = ring_reduce("grp", term(t5_gate), term(t5_up))
    inner_act = (jax.nn.gelu(gate_proj, approximate=True) * up_proj).astype(jnp.bfloat16)
    partial_ffn = jnp.dot(inner_act, down_full, preferred_element_type=jnp.float32)
    pieces_ffn = lax.all_to_all(
        partial_ffn.astype(jnp.bfloat16).reshape(16, rows, width),
        "seq",
        split_axis=0,
        concat_axis=0,
        tiled=True,
    )
    summed = jnp.sum(pieces_ffn.astype(jnp.float32), axis=0)
    encoded_local = rms_scale(local_text + summed, second_gain).astype(jnp.bfloat16)
    encoded = gather_seq(encoded_local[None])[0]

    model_dim, local_heads, triple_dim = text_proj.shape
    head_dim = triple_dim // 3
    text_qkv = jnp.dot(
        encoded, text_proj.reshape(model_dim, triple_dim), preferred_element_type=jnp.float32
    ).astype(jnp.bfloat16)
    text_valid = jnp.arange(text_total, dtype=jnp.int32) < text_lengths[0]

    image_local = image_qkv.shape[1]
    heads = image_qkv.shape[3] // head_dim
    packed = jnp.concatenate(
        [jnp.moveaxis(image_qkv[0], 1, 0).reshape(3 * image_local, -1), grad_image[0], grad_text[0]],
        axis=0,
    )
    packed = jnp.moveaxis(packed.reshape(-1, heads, head_dim), 1, 0)
    by_head = lax.all_to_all(packed, "seq", split_axis=0, concat_axis=0, tiled=True)

    def image_rows(i):
        return by_head[:, i * image_local : (i + 1) * image_local].reshape(-1, head_dim)

    upstream_text = by_head[:, 4 * image_local :].reshape(text_total, head_dim)
    upstream_text = jnp.where(text_valid[:, None], upstream_text, jnp.zeros((), jnp.bfloat16))
    image_part, text_grads = head_grads(
        text_valid,
        (
            image_rows(0),
            image_rows(1),
            image_rows(2),
            image_rows(3),
            text_qkv[:, :head_dim],
            text_qkv[:, head_dim : 2 * head_dim],
            text_qkv[:, 2 * head_dim :],
            upstream_text,
        ),
    )
    image_grad = jnp.moveaxis(image_part, 0, 1)[None, :, :, None, :]

    product = jnp.einsum(
        "tf,tc->fc", encoded, text_grads, preferred_element_type=jnp.float32
    ).astype(jnp.bfloat16)
    product = product.reshape(4, 4, -1, triple_dim)

    def dp_term(lo):
        return lambda k: lax.dynamic_slice_in_dim(product[lo : lo + 2], (d - k) % 4, 1, 1)[
            :, 0
        ].astype(jnp.float32)

    first, second = ring_reduce("dp", dp_term(0), dp_term(2))
    reduced = jnp.concatenate([first, second], axis=0).astype(jnp.bfloat16)
    half = reduced.shape[1] // 2

    def grp_term(lo):
        return lambda k: lax.dynamic_slice_in_dim(reduced[:, lo : lo + half], (g - k) % 4, 1, 0)[
            0
        ].astype(jnp.float32)

    top, bottom = ring_reduce("grp", grp_term(0), grp_term(half))
    sample_count = lax.axis_size(("grp", "dp"))
    proj_grad = jnp.concatenate([top, bottom], axis=0) / sample_count
    return (image_grad, proj_grad.reshape(-1, local_heads, triple_dim))


def solution(mesh):
    placed = (
        P(("grp", "dp"), "seq", None),
        P(("grp", "dp")),
        P(),
        P("grp", "seq"),
        P("grp", "seq"),
        P("seq", "grp"),
        P(),
        P(None, "seq", None),
        P(("grp", "dp"), "seq", None, None),
        P(("grp", "dp"), "seq", None),
        P(("grp", "dp"), "seq", None),
    )
    return jax.shard_map(
        shards,
        mesh=mesh,
        in_specs=placed,
        out_specs=(P(("grp", "dp"), None, None, "seq", None), P(("grp", "dp"), "seq", None)),
        check_vma=False,
    )
```

```python
from functools import partial

import jax
import jax.numpy as jnp
from jax import lax
from jax.experimental import pallas as pl
from jax.experimental.pallas import tpu as pltpu
from jax.sharding import PartitionSpec as P

EPSILON = 1e-06
MASKED = -1e30
LOG2E = 1.4426950408889634
HD = 128
ROWS = 128
BQ = 256
SCALE = HD**-0.5
VMEM_LIMIT = 48 * 1024 * 1024


def rms_scale(values, norm_weight):
    mean_square = jnp.mean(values * values, axis=-1, keepdims=True)
    return values * lax.rsqrt(mean_square + EPSILON) * norm_weight


def shift(x, axis, k):
    n = lax.axis_size(axis)
    return lax.ppermute(x, axis, [(i, (i + k) % n) for i in range(n)])


def shift_y(x, k):
    return lax.ppermute(
        x, "seq", [(i, (i // 8) * 8 + (i % 8 + 2 * k) % 8) for i in range(16)]
    )


def swap_seq(x, bit):
    return lax.ppermute(x, "seq", [(i, i ^ bit) for i in range(16)])


def ring_gather(x, axis):
    half = x.shape[0] // 2
    up = shift(x, axis, 1)
    down = shift(x, axis, -1)
    far_up = shift(up[:half], axis, 1)
    far_down = shift(down[half:], axis, -1)
    return x, up, down, jnp.concatenate([far_up, far_down], axis=0)


def ring_reduce(axis, up_term, down_term):
    up = up_term(1).astype(jnp.bfloat16)
    down = down_term(3).astype(jnp.bfloat16)
    for step in (2, 3):
        up = (shift(up, axis, 1).astype(jnp.float32) + up_term(step)).astype(jnp.bfloat16)
        down = (shift(down, axis, -1).astype(jnp.float32) + down_term(4 - step)).astype(
            jnp.bfloat16
        )
    up = shift(up, axis, 1).astype(jnp.float32) + up_term(0)
    down = shift(down, axis, -1).astype(jnp.float32) + down_term(0)
    return up, down


def gather_pair(x):
    return jnp.stack([x, swap_seq(x, 8)], axis=1)[:, None]


def gather_half(pair):
    k, _, _, r, c = pair.shape
    up = shift_y(pair, 1)
    down = shift_y(pair, -1)
    far = jnp.stack([shift_y(up[:, :, 0], 1), shift_y(down[:, :, 1], -1)], axis=2)
    return jnp.concatenate([pair, up, down, far], axis=1).reshape(k, 8 * r, c)


def seq_orders():
    s = lax.axis_index("seq")
    z_lo, y, core = s // 8, (s // 2) % 4, s % 2
    n = jnp.arange(16, dtype=jnp.int32)
    half, y_rel, z_rel = n // 8, (n // 2) % 4, n % 2
    y_off = jnp.where(y_rel == 0, 0, jnp.where(y_rel == 1, 3, jnp.where(y_rel == 2, 1, 2)))
    source = (z_lo ^ z_rel) * 8 + ((y + y_off) % 4) * 2 + (core ^ half)
    off = ((n // 2) % 4 - y) % 4
    rel = jnp.where(off == 0, 0, jnp.where(off == 3, 1, jnp.where(off == 1, 2, 3)))
    place = ((n % 2) ^ core) * 8 + rel * 2 + ((n // 8) ^ z_lo)
    return source, place


def dot(a, b):
    return jnp.dot(a, b, preferred_element_type=jnp.float32)


def rows_of(packed_ref, i):
    return packed_ref[:, i * ROWS : (i + 1) * ROWS, :].reshape(-1, HD)


def turned(x):
    return x.astype(jnp.float32).T.astype(jnp.bfloat16)


def image_stats_kernel(packed_ref, turn_ref, stat_ref):
    turn_ref[0] = turned(rows_of(packed_ref, 0))
    turn_ref[1] = turned(rows_of(packed_ref, 1))
    turn_ref[2] = turned(rows_of(packed_ref, 3))

    def step(i, carry):
        cols = pl.ds(pl.multiple_of(i * BQ, BQ), BQ)
        scores = dot(rows_of(packed_ref, 1), turn_ref[0, :, cols]) * (SCALE * LOG2E)
        grad_probs = dot(rows_of(packed_ref, 2), turn_ref[2, :, cols])
        top = jnp.max(scores, axis=0, keepdims=True)
        weights = jnp.exp2(scores - top)
        total = jnp.sum(weights, axis=0, keepdims=True)
        mixed = jnp.sum(weights * grad_probs, axis=0, keepdims=True)
        stat_ref[:, cols] = jnp.concatenate(
            [top, total, mixed, jnp.zeros((5, BQ), jnp.float32)], axis=0
        )
        return carry

    lax.fori_loop(0, turn_ref.shape[2] // BQ, step, 0)


def text_kernel(packed_ref, turn_ref, stat_ref, qkv_ref, up_ref, bias_ref, grads_ref, row_ref, text_row_ref):
    query_txt = qkv_ref[:, :HD]
    key_txt = qkv_ref[:, HD : 2 * HD]
    value_txt = qkv_ref[:, 2 * HD :]
    up_txt = up_ref[...]
    bias = bias_ref[:, :1]
    n_text = up_txt.shape[0]

    query_turned = turned(query_txt)
    up_turned = turned(up_txt)
    scores_i = dot(rows_of(packed_ref, 1), query_turned) * (SCALE * LOG2E)
    scores_t = dot(key_txt, query_turned) * (SCALE * LOG2E) + bias
    probs_i = dot(rows_of(packed_ref, 2), up_turned)
    probs_t = dot(value_txt, up_turned)
    top = jnp.maximum(
        jnp.max(scores_i, axis=0, keepdims=True), jnp.max(scores_t, axis=0, keepdims=True)
    )
    weights_i = jnp.exp2(scores_i - top)
    weights_t = jnp.exp2(scores_t - top)
    total = jnp.sum(weights_i, axis=0, keepdims=True) + jnp.sum(weights_t, axis=0, keepdims=True)
    inverse = 1.0 / total
    delta = inverse * (
        jnp.sum(weights_i * probs_i, axis=0, keepdims=True)
        + jnp.sum(weights_t * probs_t, axis=0, keepdims=True)
    )
    text_row_ref[...] = jnp.concatenate(
        [top + jnp.log2(total), delta, jnp.zeros((6, n_text), jnp.float32)], axis=0
    )
    soft_t = weights_t * inverse
    low_i = (weights_i * inverse * (probs_i - delta)).astype(jnp.bfloat16)
    low_t = (soft_t * (probs_t - delta)).astype(jnp.bfloat16)
    query_grad = dot(turn_ref[1], low_i) + dot(turned(key_txt), low_t)
    grads_ref[:, :HD] = (query_grad * SCALE).T.astype(jnp.bfloat16)
    key_grad = dot(low_t, query_txt)
    value_grad = dot(soft_t.astype(jnp.bfloat16), up_txt)

    def step(i, carry):
        key_grad, value_grad = carry
        cols = pl.ds(pl.multiple_of(i * BQ, BQ), BQ)
        rows = pl.ds(i * (BQ // ROWS), BQ // ROWS)
        scores = dot(key_txt, turn_ref[0, :, cols]) * (SCALE * LOG2E) + bias
        probs = dot(value_txt, turn_ref[2, :, cols])
        old = stat_ref[0:1, cols]
        top = jnp.maximum(old, jnp.max(scores, axis=0, keepdims=True))
        fade = jnp.exp2(old - top)
        weights = jnp.exp2(scores - top)
        total = stat_ref[1:2, cols] * fade + jnp.sum(weights, axis=0, keepdims=True)
        inverse = 1.0 / total
        delta = inverse * (
            stat_ref[2:3, cols] * fade + jnp.sum(weights * probs, axis=0, keepdims=True)
        )
        row_ref[:, cols] = jnp.concatenate(
            [top + jnp.log2(total), delta, jnp.zeros((6, BQ), jnp.float32)], axis=0
        )
        soft = weights * inverse
        low = (soft * (probs - delta)).astype(jnp.bfloat16)
        query_block = packed_ref[rows, 0:ROWS, :].reshape(BQ, HD)
        up_block = packed_ref[rows, 3 * ROWS : 4 * ROWS, :].reshape(BQ, HD)
        return (
            key_grad + dot(low, query_block),
            value_grad + dot(soft.astype(jnp.bfloat16), up_block),
        )

    key_grad, value_grad = lax.fori_loop(
        0, row_ref.shape[1] // BQ, step, (key_grad, value_grad)
    )
    grads_ref[:, HD : 2 * HD] = (key_grad * SCALE).astype(jnp.bfloat16)
    grads_ref[:, 2 * HD :] = value_grad.astype(jnp.bfloat16)


def image_grads_kernel(first, last, packed_ref, turn_ref, row_ref, text_row_ref, qkv_ref, up_ref, bias_ref, *rest):
    if first:
        old_ref, old_query_ref, grads_ref, sums_ref = rest
    else:
        grads_ref, sums_ref = rest
    n_steps = row_ref.shape[1] // BQ

    if first:
        sums_ref[...] = old_ref[...]
        grads_ref[0, : first * BQ] = old_query_ref[...]
    else:
        query_txt = qkv_ref[:, :HD]
        up_txt = up_ref[...]
        scores = dot(rows_of(packed_ref, 1), turned(query_txt)) * (SCALE * LOG2E)
        probs = dot(rows_of(packed_ref, 2), turned(up_txt))
        soft = jnp.exp2(scores - text_row_ref[0:1])
        low = (soft * (probs - text_row_ref[1:2])).astype(jnp.bfloat16)
        sums_ref[0] = dot(low, query_txt)
        sums_ref[1] = dot(soft.astype(jnp.bfloat16), up_txt)

    key_txt = qkv_ref[:, HD : 2 * HD]
    value_txt = qkv_ref[:, 2 * HD :]
    bias = bias_ref[:, :1]
    key_txt_turned = turned(key_txt)

    def step(i, carry):
        cols = pl.ds(pl.multiple_of(i * BQ, BQ), BQ)
        rows = pl.ds(i * (BQ // ROWS), BQ // ROWS)
        query_block = packed_ref[rows, 0:ROWS, :].reshape(BQ, HD)
        up_block = packed_ref[rows, 3 * ROWS : 4 * ROWS, :].reshape(BQ, HD)
        query_turned = turn_ref[0, :, cols]
        up_turned = turn_ref[2, :, cols]
        level = row_ref[0:1, cols]
        delta = row_ref[1:2, cols]
        scores = dot(rows_of(packed_ref, 1), query_turned) * (SCALE * LOG2E)
        probs = dot(rows_of(packed_ref, 2), up_turned)
        soft = jnp.exp2(scores - level)
        low = (soft * (probs - delta)).astype(jnp.bfloat16)
        sums_ref[0] += dot(low, query_block)
        sums_ref[1] += dot(soft.astype(jnp.bfloat16), up_block)
        scores_t = dot(key_txt, query_turned) * (SCALE * LOG2E) + bias
        probs_t = dot(value_txt, up_turned)
        low_t = (jnp.exp2(scores_t - level) * (probs_t - delta)).astype(jnp.bfloat16)
        query_grad = dot(turn_ref[1], low) + dot(key_txt_turned, low_t)
        grads_ref[0, cols] = (query_grad * SCALE).T.astype(jnp.bfloat16)
        return carry

    lax.fori_loop(first, last, step, 0)
    if last == n_steps:
        grads_ref[1] = (sums_ref[0] * SCALE).astype(jnp.bfloat16)
        grads_ref[2] = sums_ref[1].astype(jnp.bfloat16)


def call(kernel, out_shape, flops, scratch=(), outs=None):
    whole = pl.BlockSpec(memory_space=pltpu.VMEM)
    return lambda *args: pl.pallas_call(
        kernel,
        out_shape=out_shape,
        in_specs=[whole] * len(args),
        out_specs=jax.tree.map(lambda _: whole, out_shape),
        scratch_shapes=scratch,
        compiler_params=pltpu.CompilerParams(vmem_limit_bytes=VMEM_LIMIT),
        cost_estimate=pl.CostEstimate(
            flops=flops, bytes_accessed=8 * 1024 * 1024, transcendentals=0
        ),
    )(*args)


def image_stats(packed):
    n = packed.shape[0] * ROWS
    return call(
        image_stats_kernel,
        (
            jax.ShapeDtypeStruct((3, HD, n), jnp.bfloat16),
            jax.ShapeDtypeStruct((8, n), jnp.float32),
        ),
        4 * n * n * HD,
    )(packed)


def text_part(packed, turn, stats, qkv, up_txt, bias):
    n = packed.shape[0] * ROWS
    t = qkv.shape[0]
    return call(
        text_kernel,
        (
            jax.ShapeDtypeStruct((t, 3 * HD), jnp.bfloat16),
            jax.ShapeDtypeStruct((8, n), jnp.float32),
            jax.ShapeDtypeStruct((8, t), jnp.float32),
        ),
        16 * n * t * HD,
    )(packed, turn, stats, qkv, up_txt, bias)


def image_grads_first(mid, packed, turn, level, text_level, qkv, up_txt, bias):
    n = packed.shape[0] * ROWS

    def kernel(*refs):
        ins, (query_ref, sums_ref) = refs[:7], refs[7:]

        class Query:
            def __setitem__(self, at, value):
                query_ref[at[1]] = value

        image_grads_kernel(0, mid, *ins, Query(), sums_ref)

    return call(
        kernel,
        (
            jax.ShapeDtypeStruct((mid * BQ, HD), jnp.bfloat16),
            jax.ShapeDtypeStruct((2, n, HD), jnp.float32),
        ),
        10 * n * mid * BQ * HD,
    )(packed, turn, level, text_level, qkv, up_txt, bias)


def image_grads_rest(mid, packed, turn, level, text_level, qkv, up_txt, bias, sums, query):
    n = packed.shape[0] * ROWS
    return call(
        partial(image_grads_kernel, mid, n // BQ),
        jax.ShapeDtypeStruct((3, n, HD), jnp.bfloat16),
        10 * n * (n - mid * BQ) * HD,
        scratch=[pltpu.VMEM((2, n, HD), jnp.float32)],
    )(packed, turn, level, text_level, qkv, up_txt, bias, sums, query)


def shards(
    text_hidden,
    text_lengths,
    norm_gain,
    t5_gate,
    t5_up,
    t5_down,
    final_gain,
    text_proj,
    image_qkv,
    grad_image,
    grad_text,
):
    g = lax.axis_index("grp")
    d = lax.axis_index("dp")
    first_gain = norm_gain.astype(jnp.float32)
    second_gain = final_gain.astype(jnp.float32)
    local_text = text_hidden[0].astype(jnp.float32)
    rows, width = local_text.shape
    units, chunk = t5_down.shape
    source, place = seq_orders()

    def spread(x):
        parts = []
        for k in range(4):
            part = lax.dynamic_slice(x, (0, ((g + k) % 4) * chunk), (rows, chunk))
            parts.append(shift(part, "grp", k) if k else part)
        return jnp.stack(parts, axis=0)

    normed = rms_scale(local_text, first_gain).astype(jnp.bfloat16)
    pair = gather_pair(spread(normed))
    half_a = gather_half(pair)
    half_b = swap_seq(half_a, 1)

    quarter = units // 4
    mine = lax.dynamic_slice(t5_down, (d * quarter, 0), (quarter, chunk))
    mine, _ = lax.optimization_barrier((mine, pair))
    blocks = ring_gather(mine, "grp")
    blocks, _ = lax.optimization_barrier((blocks, half_a))
    wide = jnp.zeros((quarter, width), jnp.bfloat16)
    for block, off in zip(blocks, (0, 3, 1, 2)):
        wide = lax.dynamic_update_slice(wide, block, (0, ((g + off) % 4) * chunk))
    down_full = jnp.zeros((units, width), jnp.bfloat16)
    for block, off in zip(ring_gather(wide, "dp"), (0, 3, 1, 2)):
        down_full = lax.dynamic_update_slice(down_full, block, (((d + off) % 4) * quarter, 0))

    image_local = image_qkv.shape[1]
    heads = image_qkv.shape[3] // HD
    packed = jnp.concatenate(
        [jnp.moveaxis(image_qkv[0], 1, 0).reshape(3 * image_local, -1), grad_image[0], grad_text[0]],
        axis=0,
    )
    packed = jnp.moveaxis(packed.reshape(-1, heads, HD), 1, 0)
    packed, _ = lax.optimization_barrier((packed, half_a))
    by_head = lax.all_to_all(packed, "seq", split_axis=0, concat_axis=0, tiled=True)

    weight = jnp.concatenate([t5_gate, t5_up], axis=1)
    hidden_a, hidden_b = ring_reduce(
        "grp", lambda k: dot(half_a[k], weight), lambda k: dot(half_b[k], weight)
    )
    inner = []
    for hidden in (hidden_a, hidden_b):
        inner.append(
            (jax.nn.gelu(hidden[:, :units], approximate=True) * hidden[:, units:]).astype(
                jnp.bfloat16
            )
        )
    inner_act = jnp.concatenate(inner, axis=0).reshape(16, rows, units)
    inner_act = jnp.take(inner_act, place, axis=0).reshape(16 * rows, units)
    inner_act, by_head = lax.optimization_barrier((inner_act, by_head))
    partial_ffn = dot(inner_act, down_full).astype(jnp.bfloat16).reshape(16, rows, width)
    turn, stats = image_stats(by_head)
    pieces_ffn = lax.all_to_all(partial_ffn, "seq", split_axis=0, concat_axis=0, tiled=True)
    summed = jnp.sum(pieces_ffn.astype(jnp.float32), axis=0)
    encoded_local = rms_scale(local_text + summed, second_gain).astype(jnp.bfloat16)

    enc_a = gather_half(gather_pair(encoded_local[None]))[0]
    enc_b = swap_seq(enc_a, 1)
    head_proj = text_proj.reshape(width, 3 * HD)
    qkv_a = dot(enc_a, head_proj)
    text_qkv = jnp.concatenate([qkv_a, dot(enc_b, head_proj)], axis=0).astype(jnp.bfloat16)

    text_total = 16 * rows
    position = (source[:, None] * rows + jnp.arange(rows, dtype=jnp.int32)[None]).reshape(-1, 1)
    text_valid = position < text_lengths[0]
    bias = jnp.broadcast_to(jnp.where(text_valid, 0.0, MASKED), (text_total, HD))
    up_txt = jnp.take(by_head[:, 4 * ROWS :], source, axis=0).reshape(text_total, HD)
    up_txt = jnp.where(text_valid, up_txt, jnp.zeros((), jnp.bfloat16))

    text_grads, level, text_level = text_part(by_head, turn, stats, text_qkv, up_txt, bias)

    own_columns, _ = lax.optimization_barrier((encoded_local, enc_a))
    pair = gather_pair(spread(own_columns))
    cols_a = gather_half(pair)
    cols_b = swap_seq(cols_a, 1)

    shared = [text_grads] + [shift(text_grads, "grp", k) for k in (1, 2, 3)]
    mid = 4
    shared_args = (by_head, turn, level, text_level, text_qkv, up_txt, bias)
    query, sums = image_grads_first(mid, *shared_args)
    product = sum(
        lax.dot_general(
            part[k],
            shared[k][lo : lo + text_total // 2],
            (((0,), (0,)), ((), ())),
            preferred_element_type=jnp.float32,
        )
        for part, lo in ((cols_a, 0), (cols_b, text_total // 2))
        for k in range(4)
    )
    product = product.astype(jnp.bfloat16).reshape(4, -1, 3 * HD)
    total = jnp.zeros(product.shape[1:], jnp.float32)
    for k in range(4):
        part = lax.dynamic_index_in_dim(product, (d + k) % 4, 0, keepdims=False)
        total = total + (shift(part, "dp", k) if k else part).astype(jnp.float32)
    image_part = image_grads_rest(mid, *shared_args, sums, query)
    image_grad = jnp.moveaxis(image_part, 0, 1)[None, :, :, None, :]
    sample_count = lax.axis_size(("grp", "dp"))
    proj_grad = (total / sample_count).reshape(-1, 1, 3 * HD)
    return (image_grad, proj_grad)


def solution(mesh):
    placed = (
        P(("grp", "dp"), "seq", None),
        P(("grp", "dp")),
        P(),
        P("grp", "seq"),
        P("grp", "seq"),
        P("seq", "grp"),
        P(),
        P(None, "seq", None),
        P(("grp", "dp"), "seq", None, None),
        P(("grp", "dp"), "seq", None),
        P(("grp", "dp"), "seq", None),
    )
    return jax.shard_map(
        shards,
        mesh=mesh,
        in_specs=placed,
        out_specs=(P(("grp", "dp"), None, None, "seq", None), P(("grp", "dp"), "seq", None)),
        check_vma=False,
    )
```

```python
from functools import partial

import jax
import jax.numpy as jnp
from jax import lax
from jax.experimental import pallas as pl
from jax.experimental.pallas import tpu as pltpu
from jax.sharding import PartitionSpec as P

EPSILON = 1e-06
MASKED = -1e30
LOG2E = 1.4426950408889634
HD = 128
ROWS = 128
BQ = 256
SCALE = HD**-0.5
VMEM_LIMIT = 48 * 1024 * 1024


def rms_scale(values, norm_weight):
    mean_square = jnp.mean(values * values, axis=-1, keepdims=True)
    return values * lax.rsqrt(mean_square + EPSILON) * norm_weight


def shift(x, axis, k):
    n = lax.axis_size(axis)
    return lax.ppermute(x, axis, [(i, (i + k) % n) for i in range(n)])


def shift_y(x, k):
    return lax.ppermute(
        x, "seq", [(i, (i // 8) * 8 + (i % 8 + 2 * k) % 8) for i in range(16)]
    )


def swap_seq(x, bit):
    return lax.ppermute(x, "seq", [(i, i ^ bit) for i in range(16)])


def ring_reduce(axis, up_term, down_term):
    up = up_term(1).astype(jnp.bfloat16)
    down = down_term(3).astype(jnp.bfloat16)
    for step in (2, 3):
        up = (shift(up, axis, 1).astype(jnp.float32) + up_term(step)).astype(jnp.bfloat16)
        down = (shift(down, axis, -1).astype(jnp.float32) + down_term(4 - step)).astype(
            jnp.bfloat16
        )
    up = shift(up, axis, 1).astype(jnp.float32) + up_term(0)
    down = shift(down, axis, -1).astype(jnp.float32) + down_term(0)
    return up, down


def gather_pair(x):
    return jnp.stack([x, swap_seq(x, 8)], axis=1)[:, None]


def gather_half(pair):
    k, _, _, r, c = pair.shape
    blocks = [pair, shift_y(pair, 1), shift_y(pair, -1), shift_y(pair, 2)]
    return jnp.concatenate(blocks, axis=1).reshape(k, 8 * r, c)


def seq_source():
    s = lax.axis_index("seq")
    z_lo, y, core = s // 8, (s // 2) % 4, s % 2
    n = jnp.arange(16, dtype=jnp.int32)
    half, y_rel, z_rel = n // 8, (n // 2) % 4, n % 2
    y_off = jnp.where(y_rel == 0, 0, jnp.where(y_rel == 1, 3, jnp.where(y_rel == 2, 1, 2)))
    return (z_lo ^ z_rel) * 8 + ((y + y_off) % 4) * 2 + (core ^ half)


def dot(a, b):
    return jnp.dot(a, b, preferred_element_type=jnp.float32)


def rows_of(packed_ref, i):
    return packed_ref[:, i * ROWS : (i + 1) * ROWS, :].reshape(-1, HD)


def turned(x):
    return x.astype(jnp.float32).T.astype(jnp.bfloat16)


def image_stats_kernel(packed_ref, turn_ref, stat_ref):
    turn_ref[0] = turned(rows_of(packed_ref, 0))
    turn_ref[1] = turned(rows_of(packed_ref, 1))
    turn_ref[2] = turned(rows_of(packed_ref, 3))

    def step(i, carry):
        cols = pl.ds(pl.multiple_of(i * BQ, BQ), BQ)
        scores = dot(rows_of(packed_ref, 1), turn_ref[0, :, cols]) * (SCALE * LOG2E)
        grad_probs = dot(rows_of(packed_ref, 2), turn_ref[2, :, cols])
        top = jnp.max(scores, axis=0, keepdims=True)
        weights = jnp.exp2(scores - top)
        total = jnp.sum(weights, axis=0, keepdims=True)
        mixed = jnp.sum(weights * grad_probs, axis=0, keepdims=True)
        stat_ref[:, cols] = jnp.concatenate(
            [top, total, mixed, jnp.zeros((5, BQ), jnp.float32)], axis=0
        )
        return carry

    lax.fori_loop(0, turn_ref.shape[2] // BQ, step, 0)


def text_kernel(packed_ref, turn_ref, stat_ref, qkv_ref, up_ref, bias_ref, grads_ref, row_ref, text_row_ref):
    query_txt = qkv_ref[:, :HD]
    key_txt = qkv_ref[:, HD : 2 * HD]
    value_txt = qkv_ref[:, 2 * HD :]
    up_txt = up_ref[...]
    bias = bias_ref[:, :1]
    n_text = up_txt.shape[0]

    query_turned = turned(query_txt)
    up_turned = turned(up_txt)
    scores_i = dot(rows_of(packed_ref, 1), query_turned) * (SCALE * LOG2E)
    scores_t = dot(key_txt, query_turned) * (SCALE * LOG2E) + bias
    probs_i = dot(rows_of(packed_ref, 2), up_turned)
    probs_t = dot(value_txt, up_turned)
    top = jnp.maximum(
        jnp.max(scores_i, axis=0, keepdims=True), jnp.max(scores_t, axis=0, keepdims=True)
    )
    weights_i = jnp.exp2(scores_i - top)
    weights_t = jnp.exp2(scores_t - top)
    total = jnp.sum(weights_i, axis=0, keepdims=True) + jnp.sum(weights_t, axis=0, keepdims=True)
    inverse = 1.0 / total
    delta = inverse * (
        jnp.sum(weights_i * probs_i, axis=0, keepdims=True)
        + jnp.sum(weights_t * probs_t, axis=0, keepdims=True)
    )
    text_row_ref[...] = jnp.concatenate(
        [top + jnp.log2(total), delta, jnp.zeros((6, n_text), jnp.float32)], axis=0
    )
    soft_t = weights_t * inverse
    low_i = (weights_i * inverse * (probs_i - delta)).astype(jnp.bfloat16)
    low_t = (soft_t * (probs_t - delta)).astype(jnp.bfloat16)
    query_grad = dot(turn_ref[1], low_i) + dot(turned(key_txt), low_t)
    grads_ref[:, :HD] = (query_grad * SCALE).T.astype(jnp.bfloat16)
    key_grad = dot(low_t, query_txt)
    value_grad = dot(soft_t.astype(jnp.bfloat16), up_txt)

    def step(i, carry):
        key_grad, value_grad = carry
        cols = pl.ds(pl.multiple_of(i * BQ, BQ), BQ)
        rows = pl.ds(i * (BQ // ROWS), BQ // ROWS)
        scores = dot(key_txt, turn_ref[0, :, cols]) * (SCALE * LOG2E) + bias
        probs = dot(value_txt, turn_ref[2, :, cols])
        old = stat_ref[0:1, cols]
        top = jnp.maximum(old, jnp.max(scores, axis=0, keepdims=True))
        fade = jnp.exp2(old - top)
        weights = jnp.exp2(scores - top)
        total = stat_ref[1:2, cols] * fade + jnp.sum(weights, axis=0, keepdims=True)
        inverse = 1.0 / total
        delta = inverse * (
            stat_ref[2:3, cols] * fade + jnp.sum(weights * probs, axis=0, keepdims=True)
        )
        row_ref[:, cols] = jnp.concatenate(
            [top + jnp.log2(total), delta, jnp.zeros((6, BQ), jnp.float32)], axis=0
        )
        soft = weights * inverse
        low = (soft * (probs - delta)).astype(jnp.bfloat16)
        query_block = packed_ref[rows, 0:ROWS, :].reshape(BQ, HD)
        up_block = packed_ref[rows, 3 * ROWS : 4 * ROWS, :].reshape(BQ, HD)
        return (
            key_grad + dot(low, query_block),
            value_grad + dot(soft.astype(jnp.bfloat16), up_block),
        )

    key_grad, value_grad = lax.fori_loop(
        0, row_ref.shape[1] // BQ, step, (key_grad, value_grad)
    )
    grads_ref[:, HD : 2 * HD] = (key_grad * SCALE).astype(jnp.bfloat16)
    grads_ref[:, 2 * HD :] = value_grad.astype(jnp.bfloat16)


def image_grads_kernel(first, last, packed_ref, turn_ref, row_ref, text_row_ref, qkv_ref, up_ref, bias_ref, *rest):
    if first:
        old_ref, old_query_ref, grads_ref, sums_ref = rest
    else:
        grads_ref, sums_ref = rest
    n_steps = row_ref.shape[1] // BQ

    if first:
        sums_ref[...] = old_ref[...]
        grads_ref[0, : first * BQ] = old_query_ref[...]
    else:
        query_txt = qkv_ref[:, :HD]
        up_txt = up_ref[...]
        scores = dot(rows_of(packed_ref, 1), turned(query_txt)) * (SCALE * LOG2E)
        probs = dot(rows_of(packed_ref, 2), turned(up_txt))
        soft = jnp.exp2(scores - text_row_ref[0:1])
        low = (soft * (probs - text_row_ref[1:2])).astype(jnp.bfloat16)
        sums_ref[0] = dot(low, query_txt)
        sums_ref[1] = dot(soft.astype(jnp.bfloat16), up_txt)

    key_txt = qkv_ref[:, HD : 2 * HD]
    value_txt = qkv_ref[:, 2 * HD :]
    bias = bias_ref[:, :1]
    key_txt_turned = turned(key_txt)

    def step(i, carry):
        cols = pl.ds(pl.multiple_of(i * BQ, BQ), BQ)
        rows = pl.ds(i * (BQ // ROWS), BQ // ROWS)
        query_block = packed_ref[rows, 0:ROWS, :].reshape(BQ, HD)
        up_block = packed_ref[rows, 3 * ROWS : 4 * ROWS, :].reshape(BQ, HD)
        query_turned = turn_ref[0, :, cols]
        up_turned = turn_ref[2, :, cols]
        level = row_ref[0:1, cols]
        delta = row_ref[1:2, cols]
        scores = dot(rows_of(packed_ref, 1), query_turned) * (SCALE * LOG2E)
        probs = dot(rows_of(packed_ref, 2), up_turned)
        soft = jnp.exp2(scores - level)
        low = (soft * (probs - delta)).astype(jnp.bfloat16)
        sums_ref[0] += dot(low, query_block)
        sums_ref[1] += dot(soft.astype(jnp.bfloat16), up_block)
        scores_t = dot(key_txt, query_turned) * (SCALE * LOG2E) + bias
        probs_t = dot(value_txt, up_turned)
        low_t = (jnp.exp2(scores_t - level) * (probs_t - delta)).astype(jnp.bfloat16)
        query_grad = dot(turn_ref[1], low) + dot(key_txt_turned, low_t)
        grads_ref[0, cols] = (query_grad * SCALE).T.astype(jnp.bfloat16)
        return carry

    lax.fori_loop(first, last, step, 0)
    if last == n_steps:
        grads_ref[1] = (sums_ref[0] * SCALE).astype(jnp.bfloat16)
        grads_ref[2] = sums_ref[1].astype(jnp.bfloat16)


def ffn_kernel(place_ref, a_ref, b_ref, own_ref, mine_ref, up_ref, down_ref, far_a_ref, far_b_ref, out_ref, inner_ref):
    units = own_ref.shape[0]
    for n, hidden_ref in enumerate((a_ref, b_ref)):
        inner = jax.nn.gelu(hidden_ref[:, :units], approximate=True) * hidden_ref[:, units:]
        inner = inner.astype(jnp.bfloat16)
        rows = inner.shape[0] // 8
        for m in range(8):
            at = pl.multiple_of(place_ref[8 * n + m] * rows, rows)
            inner_ref[pl.ds(at, rows), :] = inner[m * rows : (m + 1) * rows]
    g, d = place_ref[16], place_ref[17]
    chunk = own_ref.shape[1]
    width = mine_ref.shape[2]

    def put(group, part, value, size, extra=0):
        at = pl.multiple_of((group % 4) * chunk + (part % 4) * width + extra, size)
        out_ref[:, pl.ds(at, size)] = dot(inner_ref[...], value).astype(jnp.bfloat16)

    for part in range(4):
        put(g, part, own_ref[:, part * width : (part + 1) * width], width)

    def step(j, carry):
        group = g + jnp.where(j == 0, 3, j)
        put(group, d, mine_ref[j], width)
        put(group, d + 3, up_ref[j], width)
        put(group, d + 1, down_ref[j], width)
        put(group, d + 2, far_a_ref[j], width // 2)
        put(group, d + 2, far_b_ref[j], width // 2, width // 2)
        return carry

    lax.fori_loop(0, 3, step, 0)


def ffn_down(place, *args):
    whole = pl.BlockSpec(memory_space=pltpu.VMEM)
    units, chunk = args[2].shape
    tokens = 2 * args[0].shape[0]
    return pl.pallas_call(
        ffn_kernel,
        out_shape=jax.ShapeDtypeStruct((tokens, 4 * chunk), jnp.bfloat16),
        in_specs=[pl.BlockSpec(memory_space=pltpu.SMEM)] + [whole] * len(args),
        out_specs=whole,
        scratch_shapes=[pltpu.VMEM((tokens, units), jnp.bfloat16)],
        compiler_params=pltpu.CompilerParams(vmem_limit_bytes=VMEM_LIMIT),
        cost_estimate=pl.CostEstimate(
            flops=8 * tokens * units * chunk, bytes_accessed=8 * 1024 * 1024, transcendentals=0
        ),
    )(place, *args)


def call(kernel, out_shape, flops, scratch=(), outs=None):
    whole = pl.BlockSpec(memory_space=pltpu.VMEM)
    return lambda *args: pl.pallas_call(
        kernel,
        out_shape=out_shape,
        in_specs=[whole] * len(args),
        out_specs=jax.tree.map(lambda _: whole, out_shape),
        scratch_shapes=scratch,
        compiler_params=pltpu.CompilerParams(vmem_limit_bytes=VMEM_LIMIT),
        cost_estimate=pl.CostEstimate(
            flops=flops, bytes_accessed=8 * 1024 * 1024, transcendentals=0
        ),
    )(*args)


def image_stats(packed):
    n = packed.shape[0] * ROWS
    return call(
        image_stats_kernel,
        (
            jax.ShapeDtypeStruct((3, HD, n), jnp.bfloat16),
            jax.ShapeDtypeStruct((8, n), jnp.float32),
        ),
        4 * n * n * HD,
    )(packed)


def text_part(packed, turn, stats, qkv, up_txt, bias):
    n = packed.shape[0] * ROWS
    t = qkv.shape[0]
    return call(
        text_kernel,
        (
            jax.ShapeDtypeStruct((t, 3 * HD), jnp.bfloat16),
            jax.ShapeDtypeStruct((8, n), jnp.float32),
            jax.ShapeDtypeStruct((8, t), jnp.float32),
        ),
        16 * n * t * HD,
    )(packed, turn, stats, qkv, up_txt, bias)


def image_grads_first(mid, packed, turn, level, text_level, qkv, up_txt, bias):
    n = packed.shape[0] * ROWS

    def kernel(*refs):
        ins, (query_ref, sums_ref) = refs[:7], refs[7:]

        class Query:
            def __setitem__(self, at, value):
                query_ref[at[1]] = value

        image_grads_kernel(0, mid, *ins, Query(), sums_ref)

    return call(
        kernel,
        (
            jax.ShapeDtypeStruct((mid * BQ, HD), jnp.bfloat16),
            jax.ShapeDtypeStruct((2, n, HD), jnp.float32),
        ),
        10 * n * mid * BQ * HD,
    )(packed, turn, level, text_level, qkv, up_txt, bias)


def image_grads_rest(mid, packed, turn, level, text_level, qkv, up_txt, bias, sums, query):
    n = packed.shape[0] * ROWS
    return call(
        partial(image_grads_kernel, mid, n // BQ),
        jax.ShapeDtypeStruct((3, n, HD), jnp.bfloat16),
        10 * n * (n - mid * BQ) * HD,
        scratch=[pltpu.VMEM((2, n, HD), jnp.float32)],
    )(packed, turn, level, text_level, qkv, up_txt, bias, sums, query)


def shards(
    text_hidden,
    text_lengths,
    norm_gain,
    t5_gate,
    t5_up,
    t5_down,
    final_gain,
    text_proj,
    image_qkv,
    grad_image,
    grad_text,
):
    g = lax.axis_index("grp")
    d = lax.axis_index("dp")
    first_gain = norm_gain.astype(jnp.float32)
    second_gain = final_gain.astype(jnp.float32)
    local_text = text_hidden[0].astype(jnp.float32)
    rows, width = local_text.shape
    units, chunk = t5_down.shape
    source = seq_source()

    def spread(x):
        parts = []
        for k in range(4):
            part = lax.dynamic_slice(x, (0, ((g + k) % 4) * chunk), (rows, chunk))
            parts.append(shift(part, "grp", k) if k else part)
        return jnp.stack(parts, axis=0)

    normed = rms_scale(local_text, first_gain).astype(jnp.bfloat16)
    tokens = spread(normed)
    pair = gather_pair(tokens)
    half_a = gather_half(pair)
    half_b = swap_seq(half_a, 1)

    image_local = image_qkv.shape[1]
    heads = image_qkv.shape[3] // HD
    packed = jnp.concatenate(
        [jnp.moveaxis(image_qkv[0], 1, 0).reshape(3 * image_local, -1), grad_image[0], grad_text[0]],
        axis=0,
    )
    packed = jnp.moveaxis(packed.reshape(-1, heads, HD), 1, 0)
    packed, _ = lax.optimization_barrier((packed, tokens))
    by_head = lax.all_to_all(packed, "seq", split_axis=0, concat_axis=0, tiled=True)

    quarter = chunk // 4
    mine = lax.dynamic_slice(t5_down, (0, d * quarter), (units, quarter))
    mine, _ = lax.optimization_barrier((mine, pair))
    mine = jnp.stack([shift(mine, "grp", k) for k in (1, -1, 2)], axis=0)
    down_up = shift(mine, "dp", 1)
    down_down = shift(mine, "dp", -1)
    down_far_a = shift(down_up[:, :, : quarter // 2], "dp", 1)
    down_far_b = shift(down_down[:, :, quarter // 2 :], "dp", -1)

    weight = jnp.concatenate([t5_gate, t5_up], axis=1)
    hidden_a, hidden_b = ring_reduce(
        "grp", lambda k: dot(half_a[k], weight), lambda k: dot(half_b[k], weight)
    )
    at = jnp.concatenate([source, jnp.stack([g, d])]).astype(jnp.int32)
    partial_ffn = ffn_down(
        at, hidden_a, hidden_b, t5_down, mine, down_up, down_down, down_far_a, down_far_b
    ).reshape(16, rows, width)
    by_head, partial_ffn = lax.optimization_barrier((by_head, partial_ffn))
    turn, stats = image_stats(by_head)
    pieces_ffn = lax.all_to_all(partial_ffn, "seq", split_axis=0, concat_axis=0, tiled=True)
    pieces_ffn, turn, stats = lax.optimization_barrier((pieces_ffn, turn, stats))
    summed = jnp.sum(pieces_ffn.astype(jnp.float32), axis=0)
    encoded_local = rms_scale(local_text + summed, second_gain).astype(jnp.bfloat16)

    enc_pair = gather_pair(encoded_local[None])
    enc_a = gather_half(enc_pair)[0]
    enc_b = swap_seq(enc_a, 1)
    head_proj = text_proj.reshape(width, 3 * HD)
    qkv_a = dot(enc_a, head_proj)
    text_qkv = jnp.concatenate([qkv_a, dot(enc_b, head_proj)], axis=0).astype(jnp.bfloat16)

    text_total = 16 * rows
    position = (source[:, None] * rows + jnp.arange(rows, dtype=jnp.int32)[None]).reshape(-1, 1)
    text_valid = position < text_lengths[0]
    bias = jnp.broadcast_to(jnp.where(text_valid, 0.0, MASKED), (text_total, HD))
    up_txt = jnp.take(by_head[:, 4 * ROWS :], source, axis=0).reshape(text_total, HD)
    up_txt = jnp.where(text_valid, up_txt, jnp.zeros((), jnp.bfloat16))

    text_grads, level, text_level = text_part(by_head, turn, stats, text_qkv, up_txt, bias)

    own_columns, _ = lax.optimization_barrier((encoded_local, enc_pair))
    own_columns, _ = lax.optimization_barrier((spread(own_columns), enc_a))
    own_pair, _ = lax.optimization_barrier((gather_pair(own_columns), enc_b))
    cols_a = gather_half(own_pair)
    cols_b = swap_seq(cols_a, 1)

    shared = [text_grads] + [shift(text_grads, "grp", k) for k in (1, 2, 3)]
    mid = 4
    shared_args = (by_head, turn, level, text_level, text_qkv, up_txt, bias)
    query, sums = image_grads_first(mid, *shared_args)
    product = sum(
        lax.dot_general(
            part[k],
            shared[k][lo : lo + text_total // 2],
            (((0,), (0,)), ((), ())),
            preferred_element_type=jnp.float32,
        )
        for part, lo in ((cols_a, 0), (cols_b, text_total // 2))
        for k in range(4)
    )
    product = product.astype(jnp.bfloat16).reshape(4, -1, 3 * HD)
    total = jnp.zeros(product.shape[1:], jnp.float32)
    for k in range(4):
        part = lax.dynamic_index_in_dim(product, (d + k) % 4, 0, keepdims=False)
        total = total + (shift(part, "dp", k) if k else part).astype(jnp.float32)
    image_part = image_grads_rest(mid, *shared_args, sums, query)
    image_grad = jnp.moveaxis(image_part, 0, 1)[None, :, :, None, :]
    sample_count = lax.axis_size(("grp", "dp"))
    proj_grad = (total / sample_count).reshape(-1, 1, 3 * HD)
    return (image_grad, proj_grad)


def solution(mesh):
    placed = (
        P(("grp", "dp"), "seq", None),
        P(("grp", "dp")),
        P(),
        P("grp", "seq"),
        P("grp", "seq"),
        P("seq", "grp"),
        P(),
        P(None, "seq", None),
        P(("grp", "dp"), "seq", None, None),
        P(("grp", "dp"), "seq", None),
        P(("grp", "dp"), "seq", None),
    )
    return jax.shard_map(
        shards,
        mesh=mesh,
        in_specs=placed,
        out_specs=(P(("grp", "dp"), None, None, "seq", None), P(("grp", "dp"), "seq", None)),
        check_vma=False,
    )
```
